32 devices in a mesh: table: 16 (over z, y, x), mp: 2 (over core).
Axes of the slice: x: 2, y: 2, z: 4, core: 2. Of those that a mesh axis runs over, the one named last changes fastest.
Arguments:
- hash_tables: bfloat16 [2, 16384, 4096], P(None, 'table', 'mp'), may hold values from -6 to 6
- byte_table: bfloat16 [256, 4096], P(None, 'mp'), may hold values from -6 to 6
- byte_ids: int32 [4096], P('table'), may hold values from 0 to 255
- hash_owner: int32 [2, 4096, 1], P(None, 'table'), may hold values from 0 to 15; in each aligned block of 256 rows (0 to 255, 256 to 511, ..., all dimensions but the last counted through in order) at most 32 rows name the same one
- hash_offset: int32 [2, 4096], P(None, 'table'), may hold values from 0 to 1023
- gain: float32 [4096], replicated, may hold values from 0.25 to 1.75
- proj_weight: bfloat16 [4096, 4096], P('table', 'mp'), may hold values from -0.09375 to 0.09375
- cotangent: bfloat16 [4096, 4096], P('table', 'mp'), may hold values from -6 to 6
Outputs:
- projected: bfloat16 [4096, 4096], P('table', 'mp')
- table_grads: bfloat16 [2, 16384, 4096], P(None, 'table', 'mp')
The draws below stay inside these ranges and needn't reach their ends.
Inputs may be any that keep to these rules, and one draw needn't show every extreme that they name: `hash_owner`: within the 256 bytes of one device and one table, no owner is named more than 32 times, a bound that some of these blocks reach.
All inputs are finite; a program needn't handle non-finite values.
Results may differ from the reference program's by a relative error of at most 0.0058.
Values may be sent and summed in bfloat16 or wider, within the bound.
A program may use at most 128 MiB of HBM per device.

```python
import math
import jax
import jax.numpy as jnp
import numpy as np
from jax import lax

D = 4096
NGRAMS = 2
ROWS_DEV = 1024
VOCAB = 256
TOK_DEV = 256
TOKENS = 4096
ROWS = 16384
CAP = 32
N_TABLE = 16


def plant(drawn, own_key, least, largest):
    spot = [jax.random.randint(jax.random.fold_in(own_key, axis), (), 0, length) for axis, length in enumerate(drawn.shape)]
    longest = drawn.shape.index(max(drawn.shape))
    beside = spot[:longest] + [(spot[longest] + 1) % drawn.shape[longest]] + spot[longest + 1:]
    return drawn.at[tuple(spot)].set(least).at[tuple(beside)].set(largest)


def steps_of(rng, dims, split, least, top_value):
    level = 1.0
    for dim, parts in split:
        steps = jax.random.uniform(jax.random.fold_in(jax.random.fold_in(rng, 6), dim), (parts,), jnp.float32, least / len(split), top_value / len(split))
        level = level * jnp.repeat(jnp.exp(steps), dims[dim] // parts).reshape((-1,) + (1,) * (len(dims) - 1 - dim))
    return level


def cumulative_ranks(number_of, lean):
    portions = [(1 << 20) // math.isqrt(grade ** lean) + 1 for grade in range(1, number_of + 1)]
    deviation = 1 + sum(portions) // (1 << 30)
    return np.cumsum(np.array([max(1, weight // deviation) for weight in portions]))


def ranked(stream_key, dims, amount, slope):
    table = cumulative_ranks(amount, slope)
    lot = jax.random.randint(jax.random.fold_in(stream_key, 1), dims, 0, int(table[amount - 1]))
    standing = jnp.searchsorted(jnp.asarray(table, jnp.int32), lot, side="right")
    return jax.random.permutation(jax.random.fold_in(stream_key, 2), amount)[standing].astype(jnp.int32)


def assign_block(stream_key, own, number, rows, amount, top, limit, lean):
    sequence = jax.random.permutation(stream_key, amount)
    packed, usual = load_shares(amount, rows * top, limit, lean, True), load_shares(amount, rows * top, limit, lean, False)
    places = jnp.arange(amount)

    def named(lengths, turn):
        used = int((lengths > 0).sum())
        fixed = max(1, used // 4)
        moved = fixed + (places - fixed + turn * (used - fixed)) % max(1, amount - fixed)
        return jnp.zeros((amount,), jnp.int32).at[sequence[jnp.where(places < fixed, places, moved)]].set(jnp.asarray(lengths, jnp.int32))

    lengths = jnp.where(number % 4 == 0, named(packed, number // 4), named(usual, number - number // 4 - 1))
    mixed = jax.random.permutation(jax.random.fold_in(own, 3), amount)
    donor, receiver = mixed[0:amount // 2 * 2:2], mixed[1:amount // 2 * 2:2]
    room = jnp.minimum(lengths[donor] - 1, limit - lengths[receiver]) // 2
    room = jnp.where((donor == sequence[0]) | (receiver == sequence[0]) | (lengths[receiver] == 0), 0, jnp.maximum(room, 0))
    moved = jax.random.randint(jax.random.fold_in(own, 4), (amount // 2,), 0, 1 << 20) % (room + 1)
    lengths = lengths.at[donor].add(-moved).at[receiver].add(moved)
    members = jnp.searchsorted(jnp.cumsum(lengths), jnp.arange(rows * top), side="right").astype(jnp.int32)
    grid = members.reshape(top, rows).T
    grid = grid[jax.random.permutation(jax.random.fold_in(own, 1), rows)]
    turn = jax.random.randint(jax.random.fold_in(own, 2), (rows, 1), 0, top)
    return jnp.take_along_axis(grid, (jnp.arange(top)[None, :] + turn) % top, axis=1)


def load_shares(number_of, total, limit, slope, full):
    portions = [(1 << 20) // math.isqrt(grade ** slope) + 1 for grade in range(1, number_of + 1)]
    largest = limit if full else min(limit, max(-(-total // number_of), total * portions[0] // sum(portions)))
    least = 1 if total - largest >= number_of - 1 else 0
    counts, surplus = [largest] + [least] * (number_of - 1), total - largest - least * (number_of - 1)
    while surplus > 0:
        movable = [i for i in range(1, number_of) if counts[i] < largest] or [i for i in range(1, number_of) if counts[i] < limit]
        mass, remaining = sum([portions[i] for i in movable]), surplus
        for i in movable:
            extra = min(limit - counts[i], max(1, remaining * portions[i] // mass), surplus)
            counts[i] = counts[i] + extra
            surplus = surplus - extra
    return np.array(counts)


def noise(stream_key, shape, scale, reach, pieces=(), kind=jnp.bfloat16):
    array = jax.random.normal(stream_key, shape, jnp.float32) * scale
    if len(pieces) > 0:
        array = steps_of(stream_key, shape, pieces, -0.22, 0.18) * array
    return jnp.clip(array, min=-reach, max=reach).astype(kind)


def setup_inputs(seed: int = 0) -> dict:
    keys = jax.random.split(jax.random.key(seed), 9)
    hash_tables = noise(keys[0], (NGRAMS, ROWS, D), 1.0, 6.0, ((1, 16), (2, 2)))
    byte_table = noise(keys[1], (VOCAB, D), 1.0, 6.0, ((1, 2),))
    byte_ids = plant(ranked(keys[2], (TOKENS,), VOCAB, 2), jax.random.fold_in(keys[2], 3), 0, VOCAB - 1).astype(jnp.int32)
    hash_owner_keys = jax.random.split(jax.random.fold_in(keys[3], 1), NGRAMS * TOKENS // TOK_DEV)
    hash_owner_turns = jax.random.permutation(jax.random.fold_in(keys[3], 3), NGRAMS * TOKENS // TOK_DEV)
    hash_owner = jax.vmap(lambda own, number: assign_block(jax.random.fold_in(keys[3], 2), own, number, TOK_DEV, N_TABLE, 1, CAP, 2))(hash_owner_keys, hash_owner_turns).reshape((NGRAMS, TOKENS, 1))
    hash_offset = plant(jax.random.randint(keys[4], (NGRAMS, TOKENS), 0, ROWS_DEV), jax.random.fold_in(keys[4], 1), 0, ROWS_DEV - 1).astype(jnp.int32)
    gain = jnp.clip(1.0 + 0.15 * jax.random.normal(keys[5], (D,), jnp.float32), 0.25, 1.75)
    proj_weight = noise(keys[6], (D, D), D ** -0.5, 0.09375, ((0, 16), (1, 2)))
    cotangent = noise(keys[7], (TOKENS, D), 1.0, 6.0, ((0, 16), (1, 2)))
    return {"hash_tables": hash_tables, "byte_table": byte_table, "byte_ids": byte_ids, "hash_owner": hash_owner, "hash_offset": hash_offset, "gain": gain, "proj_weight": proj_weight, "cotangent": cotangent}


eps = 1e-05

def reference(hash_tables, byte_table, byte_ids, hash_owner, hash_offset, gain, proj_weight, cotangent):
    hashed = (hash_owner[:, :, 0] * ROWS_DEV + hash_offset).astype(jnp.int32)
    summed = byte_table[byte_ids].astype(jnp.float32)
    for k in range(NGRAMS):
        summed = summed + hash_tables[k][hashed[k]].astype(jnp.float32)
    embedded = summed.astype(jnp.bfloat16)
    values = embedded.astype(jnp.float32)
    scale = lax.rsqrt(lax.optimization_barrier(jnp.mean(values * values, axis=1, keepdims=True)) + eps)
    normed = (values * scale * gain[None, :]).astype(jnp.bfloat16)
    projected = jnp.dot(normed, proj_weight, preferred_element_type=jnp.float32).astype(jnp.bfloat16)
    dnormed = lax.dot_general(cotangent, proj_weight, (((1,), (1,)), ((), ())), preferred_element_type=jnp.float32)
    scaled = dnormed * gain[None, :]
    inner = lax.optimization_barrier(jnp.mean(values * scaled, axis=1, keepdims=True))
    dembed = (scale * scaled - values * scale * scale * scale * inner).astype(jnp.bfloat16)
    grads = []
    for k in range(NGRAMS):
        total = jnp.zeros((ROWS, D), jnp.float32).at[hashed[k]].add(dembed.astype(jnp.float32))
        grads.append(total.astype(jnp.bfloat16))
    return (projected, jnp.stack(grads))
```

```python
import functools

import jax
import jax.numpy as jnp
from jax import lax
from jax.experimental import pallas as pl
from jax.experimental.pallas import tpu as pltpu
from jax.sharding import PartitionSpec as P

eps = 1e-05
MESH = pl.DeviceIdType.MESH
ANY = pl.BlockSpec(memory_space=pl.ANY)


def slot_rank(owner, groups):
    marks = (owner[:, None] == jnp.arange(groups, dtype=jnp.int32)[None, :]).astype(jnp.int32)
    before = jnp.cumsum(marks, axis=0) - marks
    return jnp.sum(before * marks, axis=1)


def greet_table(n):
    me = lax.axis_index("table")
    barrier = pltpu.get_barrier_semaphore()
    for j in range(1, n):
        pl.semaphore_signal(
            barrier, inc=1, device_id={"table": lax.rem(me + j, n)}, device_id_type=MESH
        )
    pl.semaphore_wait(barrier, n - 1)


def start_exchange(n, src, dst, send, recv, window):
    me = lax.axis_index("table")
    copies = []
    for j in range(1, n):
        to = lax.rem(me + j, n)
        copy = pltpu.make_async_remote_copy(
            src_ref=window(src, to),
            dst_ref=window(dst, me),
            send_sem=send.at[j],
            recv_sem=recv.at[j],
            device_id={"table": to},
            device_id_type=MESH,
        )
        copy.start()
        copies.append(copy)
    return copies


def own_block(src, dst, hold, sem, window):
    me = lax.axis_index("table")
    load = pltpu.make_async_copy(window(src, me), hold, sem.at[0])
    load.start()
    load.wait()
    store = pltpu.make_async_copy(hold, window(dst, me), sem.at[1])
    store.start()
    return store


def first_window(ref, d):
    return ref.at[d]


def second_window(ref, d):
    return ref.at[:, d]


def exchange_kernel(n, window, x_ref, y_ref, hold, send, recv, local):
    greet_table(n)
    copies = start_exchange(n, x_ref, y_ref, send, recv, window)
    store = own_block(x_ref, y_ref, hold, local, window)
    store.wait()
    for copy in copies:
        copy.wait()


def exchange(x, n, window, collective_id):
    block = x.shape[1:] if window is first_window else x.shape[:1] + x.shape[2:]
    return pl.pallas_call(
        functools.partial(exchange_kernel, n, window),
        out_shape=jax.ShapeDtypeStruct(x.shape, x.dtype),
        in_specs=[ANY],
        out_specs=ANY,
        scratch_shapes=[
            pltpu.VMEM(block, x.dtype),
            pltpu.SemaphoreType.DMA((n,)),
            pltpu.SemaphoreType.DMA((n,)),
            pltpu.SemaphoreType.DMA((2,)),
        ],
        compiler_params=pltpu.CompilerParams(
            collective_id=collective_id, has_side_effects=True
        ),
    )(x)


def factors(n):
    major = 1
    while major * major < n:
        major *= 2
    return major, n // major


def snake(i):
    return (i // 2) * 2 + (i % 2 + i // 2) % 2


def gather_steps(n):
    major, minor = factors(n)
    total = 0
    for first, second in ((major, minor), (minor, major)):
        total += 2 * (first // 2) + first * 2 * (second // 2)
    return total


def start_gather(n, w_ref, out_ref, send, recv):
    major, minor = factors(n)
    me = lax.axis_index("table")
    row, place = me // minor, snake(me % minor)
    depth = w_ref.shape[0]
    half = depth // 2
    spot = [0]
    started = []

    def device(r, p):
        return lax.rem(r + major, major) * minor + snake(lax.rem(p + minor, minor))

    def send_block(origin, own, part, piece, to):
        size = half if piece is None else half // 2
        offset = part * half + (0 if piece is None else piece * size)
        at = pl.ds(pl.multiple_of(origin * depth + offset, size), size)
        src = w_ref.at[pl.ds(offset, size)] if own else out_ref.at[at]
        copy = pltpu.make_async_remote_copy(
            src_ref=src,
            dst_ref=out_ref.at[at],
            send_sem=send.at[spot[0]],
            recv_sem=recv.at[spot[0]],
            device_id={"table": to},
            device_id_type=MESH,
        )
        spot[0] += 1
        copy.start()
        started.append(copy)
        return copy

    class Chain:
        def __init__(self, part, ring, other, own):
            self.part, self.ring, self.other, self.own = part, ring, other, own
            self.size = major if ring == 0 else minor
            self.step = 0
            self.flight = None

        def at(self, shift):
            if self.ring == 0:
                return device(row + shift, self.other)
            return device(self.other, place + shift)

        def to(self, shift):
            if self.ring == 0:
                return device(row + shift, place)
            return device(row, place + shift)

        def go(self):
            last = self.step + 1 == self.size // 2
            pieces = (0, 1) if last else (None, None)
            own = self.own and self.step == 0
            self.flight = (
                send_block(self.at(-self.step), own, self.part, pieces[0], self.to(1)),
                send_block(self.at(self.step), own, self.part, pieces[1], self.to(-1)),
            )
            self.step += 1

        def arrive(self):
            for copy in self.flight:
                copy.wait_recv()
            if self.step < self.size // 2:
                self.go()

    firsts = [Chain(0, 0, place, True), Chain(1, 1, row, True)]
    seconds = [[Chain(0, 1, row, True)], [Chain(1, 0, place, True)]]
    for part in (0, 1):
        firsts[part].go()
    for part in (0, 1):
        seconds[part][0].go()
    for step in range(1, max(major, minor) // 2 + 1):
        for part in (0, 1):
            ring = (major, minor)[part]
            if step > ring // 2:
                continue
            firsts[part].arrive()
            shifts = (-step, step) if step < ring // 2 else (step,)
            for shift in shifts:
                if part == 0:
                    chain = Chain(0, 1, lax.rem(row + shift + major, major), False)
                else:
                    chain = Chain(1, 0, lax.rem(place + shift + minor, minor), False)
                chain.go()
                seconds[part].append(chain)
    for step in range(1, max(major, minor) // 2 + 1):
        for pair in zip(*seconds) if major == minor else [c for c in seconds]:
            for chain in pair:
                if step <= chain.size // 2:
                    chain.arrive()
    return started


def gather_kernel(n, w_ref, x_ref, w_out, y_ref, hold_w, hold_x, ws, wr, xs, xr, local):
    greet_table(n)
    copies = start_exchange(n, x_ref, y_ref, xs, xr, second_window)
    store = own_block(x_ref, y_ref, hold_x, local, second_window)
    me = lax.axis_index("table")
    depth = w_ref.shape[0]
    load = pltpu.make_async_copy(w_ref, hold_w, local.at[2])
    load.start()
    started = start_gather(n, w_ref, w_out, ws, wr)
    load.wait()
    put = pltpu.make_async_copy(
        hold_w, w_out.at[pl.ds(pl.multiple_of(me * depth, depth), depth)], local.at[3]
    )
    put.start()
    store.wait()
    put.wait()
    for copy in copies:
        copy.wait()
    for copy in started:
        copy.wait_send()


def gather_and_exchange(w, x, n, collective_id):
    steps = gather_steps(n)
    return pl.pallas_call(
        functools.partial(gather_kernel, n),
        out_shape=(
            jax.ShapeDtypeStruct((n * w.shape[0], w.shape[1]), w.dtype),
            jax.ShapeDtypeStruct(x.shape, x.dtype),
        ),
        in_specs=[ANY, ANY],
        out_specs=(ANY, ANY),
        scratch_shapes=[
            pltpu.VMEM(w.shape, w.dtype),
            pltpu.VMEM(x.shape[:1] + x.shape[2:], x.dtype),
            pltpu.SemaphoreType.DMA((steps,)),
            pltpu.SemaphoreType.DMA((steps,)),
            pltpu.SemaphoreType.DMA((n,)),
            pltpu.SemaphoreType.DMA((n,)),
            pltpu.SemaphoreType.DMA((4,)),
        ],
        compiler_params=pltpu.CompilerParams(
            collective_id=collective_id, has_side_effects=True
        ),
    )(w, x)


def greet_pair():
    other = 1 - lax.axis_index("mp")
    barrier = pltpu.get_barrier_semaphore()
    pl.semaphore_signal(barrier, inc=1, device_id={"mp": other}, device_id_type=MESH)
    pl.semaphore_wait(barrier, 1)
    return other


def join_kernel(x_ref, full_ref, send, recv, local):
    other = greet_pair()
    width = x_ref.shape[1]
    window = full_ref.at[:, pl.ds(pl.multiple_of((1 - other) * width, width), width)]
    copy = pltpu.make_async_remote_copy(
        src_ref=x_ref,
        dst_ref=window,
        send_sem=send,
        recv_sem=recv,
        device_id={"mp": other},
        device_id_type=MESH,
    )
    copy.start()
    keep = pltpu.make_async_copy(x_ref, window, local)
    keep.start()
    keep.wait()
    copy.wait()


def join_halves(x, collective_id):
    return pl.pallas_call(
        join_kernel,
        out_shape=jax.ShapeDtypeStruct((x.shape[0], 2 * x.shape[1]), x.dtype),
        in_specs=[pl.BlockSpec(memory_space=pltpu.VMEM)],
        out_specs=ANY,
        scratch_shapes=[pltpu.SemaphoreType.DMA] * 3,
        compiler_params=pltpu.CompilerParams(
            collective_id=collective_id, has_side_effects=True
        ),
    )(x)


def swap_kernel(part_ref, side_ref, part_out, side_out, send, recv):
    other = greet_pair()
    width = part_out.shape[1]
    copies = []
    pairs = (
        (part_ref.at[:, pl.ds(pl.multiple_of(other * width, width), width)], part_out),
        (side_ref, side_out),
    )
    for i, (src, dst) in enumerate(pairs):
        copy = pltpu.make_async_remote_copy(
            src_ref=src,
            dst_ref=dst,
            send_sem=send.at[i],
            recv_sem=recv.at[i],
            device_id={"mp": other},
            device_id_type=MESH,
        )
        copy.start()
        copies.append(copy)
    for copy in copies:
        copy.wait()


def swap_halves(part, side, collective_id):
    return pl.pallas_call(
        swap_kernel,
        out_shape=(
            jax.ShapeDtypeStruct((part.shape[0], part.shape[1] // 2), part.dtype),
            jax.ShapeDtypeStruct(side.shape, side.dtype),
        ),
        in_specs=[ANY, ANY],
        out_specs=(ANY, ANY),
        scratch_shapes=[pltpu.SemaphoreType.DMA((2,)), pltpu.SemaphoreType.DMA((2,))],
        compiler_params=pltpu.CompilerParams(
            collective_id=collective_id, has_side_effects=True
        ),
    )(part, side)


def on_device(
    hash_tables, byte_table, byte_ids, hash_owner, hash_offset, gain, proj_weight, cotangent
):
    groups = lax.axis_size("table")
    half = lax.axis_index("mp")
    ngram, rows_dev, width = hash_tables.shape
    tokens = byte_ids.shape[0]
    full_width = gain.shape[0]
    capacity = 2 * tokens // groups
    span = groups * capacity
    places = jnp.arange(span, dtype=jnp.int32)
    marks = []
    requests = []
    for k in range(ngram):
        owner = hash_owner[k, :, 0]
        slot = owner * capacity + slot_rank(owner, groups)
        mark = slot[:, None] == places[None, :]
        marks.append(mark)
        wanted = jnp.sum(jnp.where(mark, hash_offset[k][:, None] + 1, 0), axis=0) - 1
        requests.append(wanted.reshape(groups, capacity))
    stacked = jnp.stack(requests, axis=1)
    lanes = -(-capacity // 128) * 128
    levels = -(-ngram // 8) * 8
    stacked = jnp.pad(stacked, ((0, 0), (0, levels - ngram), (0, lanes - capacity)))
    asked = exchange(stacked, groups, first_window, 0)[:, :ngram, :capacity]
    asked = jnp.transpose(asked, (1, 0, 2)).reshape(ngram, span)
    rows = jnp.arange(rows_dev, dtype=jnp.int32)
    hits = (asked[:, :, None] == rows[None, None, :]).astype(jnp.bfloat16)
    looked = lax.dot_general(
        hits, hash_tables, (((2,), (1,)), ((0,), (0,))), preferred_element_type=jnp.float32
    ).astype(jnp.bfloat16)
    weight, fetched = gather_and_exchange(
        proj_weight, looked.reshape(ngram, groups, capacity, width), groups, 1
    )

    mark = jnp.concatenate(marks, axis=1).astype(jnp.bfloat16)
    codes = jnp.arange(byte_table.shape[0], dtype=jnp.int32)
    picks = (byte_ids[:, None] == codes[None, :]).astype(jnp.bfloat16)
    summed = jnp.dot(picks, byte_table, preferred_element_type=jnp.float32)
    summed = summed + jnp.dot(
        mark, fetched.reshape(ngram * span, width), preferred_element_type=jnp.float32
    )
    embedded_half = summed.astype(jnp.bfloat16)
    embedded = join_halves(embedded_half, 2)
    full = embedded.astype(jnp.float32)
    total = jnp.sum(full * full, axis=1)
    scale = lax.rsqrt(total / full_width + eps)[:, None]
    normed = (full * scale * gain[None, :]).astype(jnp.bfloat16)
    partial_grad = lax.dot_general(
        cotangent, weight, (((1,), (1,)), ((), ())), preferred_element_type=jnp.float32
    )
    inner_part = jnp.sum(full * (partial_grad * gain[None, :]), axis=1, keepdims=True)
    other_grad, other_inner = swap_halves(
        partial_grad, jnp.broadcast_to(inner_part, (tokens, 128)), 3
    )
    values = embedded_half.astype(jnp.float32)
    gain_half = lax.dynamic_slice_in_dim(gain, half * width, width)
    own_grad = lax.dynamic_slice_in_dim(partial_grad, half * width, width, axis=1)
    scaled = (own_grad + other_grad) * gain_half[None, :]
    inner = (inner_part + other_inner[:, :1]) / full_width
    dembed = (scale * scaled - values * scale * scale * scale * inner).astype(jnp.bfloat16)
    outgoing = lax.dot_general(
        mark, dembed, (((0,), (0,)), ((), ())), preferred_element_type=jnp.float32
    ).astype(jnp.bfloat16)
    arrived = exchange(
        outgoing.reshape(ngram, groups, capacity, width), groups, second_window, 4
    )
    grads = lax.dot_general(
        hits,
        arrived.reshape(ngram, span, width),
        (((1,), (1,)), ((0,), (0,))),
        preferred_element_type=jnp.float32,
    ).astype(jnp.bfloat16)
    projected = jnp.dot(normed, weight, preferred_element_type=jnp.float32).astype(jnp.bfloat16)
    return (projected, grads)


def solution(mesh):
    return jax.shard_map(
        on_device,
        mesh=mesh,
        in_specs=(
            P(None, "table", "mp"),
            P(None, "mp"),
            P("table"),
            P(None, "table", None),
            P(None, "table"),
            P(),
            P("table", "mp"),
            P("table", "mp"),
        ),
        out_specs=(P("table", "mp"), P(None, "table", "mp")),
        check_vma=False,
    )
```

```python
import functools

import jax
import jax.numpy as jnp
from jax import lax
from jax.experimental import pallas as pl
from jax.experimental.pallas import tpu as pltpu
from jax.sharding import PartitionSpec as P

eps = 1e-05
MESH = pl.DeviceIdType.MESH
ANY = pl.BlockSpec(memory_space=pl.ANY)


def slot_rank(owner, groups):
    marks = (owner[:, None] == jnp.arange(groups, dtype=jnp.int32)[None, :]).astype(jnp.int32)
    before = jnp.cumsum(marks, axis=0) - marks
    return jnp.sum(before * marks, axis=1)


def greet_table(n):
    me = lax.axis_index("table")
    barrier = pltpu.get_barrier_semaphore()
    for j in range(1, n):
        pl.semaphore_signal(
            barrier, inc=1, device_id={"table": lax.rem(me + j, n)}, device_id_type=MESH
        )
    pl.semaphore_wait(barrier, n - 1)


def exchange_copies(n, src, dst, send, recv, window):
    me = lax.axis_index("table")
    copies = []
    for j in range(1, n):
        to = lax.rem(me + j, n)
        copy = pltpu.make_async_remote_copy(
            src_ref=window(src, to),
            dst_ref=window(dst, me),
            send_sem=send.at[j],
            recv_sem=recv.at[j],
            device_id={"table": to},
            device_id_type=MESH,
        )
        copies.append(copy)
    return copies


def own_block(src, dst, hold, sem, window):
    me = lax.axis_index("table")
    load = pltpu.make_async_copy(window(src, me), hold, sem.at[0])
    load.start()
    load.wait()
    store = pltpu.make_async_copy(hold, window(dst, me), sem.at[1])
    store.start()
    return store


def first_window(ref, d):
    return ref.at[d]


def second_window(ref, d):
    return ref.at[:, d]


def exchange_kernel(n, window, x_ref, y_ref, hold, send, recv, local):
    greet_table(n)
    copies = exchange_copies(n, x_ref, y_ref, send, recv, window)
    for copy in copies:
        copy.start()
    store = own_block(x_ref, y_ref, hold, local, window)
    store.wait()
    for copy in copies:
        copy.wait()


def exchange(x, n, window, collective_id):
    block = x.shape[1:] if window is first_window else x.shape[:1] + x.shape[2:]
    return pl.pallas_call(
        functools.partial(exchange_kernel, n, window),
        out_shape=jax.ShapeDtypeStruct(x.shape, x.dtype),
        in_specs=[ANY],
        out_specs=ANY,
        scratch_shapes=[
            pltpu.VMEM(block, x.dtype),
            pltpu.SemaphoreType.DMA((n,)),
            pltpu.SemaphoreType.DMA((n,)),
            pltpu.SemaphoreType.DMA((2,)),
        ],
        compiler_params=pltpu.CompilerParams(
            collective_id=collective_id, has_side_effects=True
        ),
    )(x)


def factors(n):
    major = 1
    while major * major < n:
        major *= 2
    return major, n // major


def snake(i):
    return (i // 2) * 2 + (i % 2 + i // 2) % 2


def gather_steps(n):
    major, minor = factors(n)
    return 2 * (major - 1) + (2 * major - 1) * 2 * (minor // 2)


def start_gather(n, w_ref, out_ref, send, recv, between):
    major, minor = factors(n)
    me = lax.axis_index("table")
    row, place = me // minor, snake(me % minor)
    depth = w_ref.shape[0]
    spot = [0]
    sends = []

    def always(body):
        body()

    def when(condition):
        return always if condition is None else pl.when(condition)

    def on_ring(r, shift):
        return r * minor + snake(lax.rem(place + shift + minor, minor))

    def copy_of(origin, own, piece, to):
        size = depth if piece is None else depth // 2
        offset = 0 if piece is None else piece * size
        at = pl.ds(pl.multiple_of(origin * depth + offset, size), size)
        copy = pltpu.make_async_remote_copy(
            src_ref=w_ref.at[pl.ds(offset, size)] if own else out_ref.at[at],
            dst_ref=out_ref.at[at],
            send_sem=send.at[spot[0]],
            recv_sem=recv.at[spot[0]],
            device_id={"table": to},
            device_id_type=MESH,
        )
        spot[0] += 1
        return copy

    def line_copy(step, way):
        origin = lax.rem(row - way * (step - 1) + major, major)
        to = lax.rem(row + way + major, major)
        return copy_of(
            origin * minor + me % minor, step == 1, None, to * minor + me % minor
        )

    def has(shift):
        return jnp.logical_and(row + shift >= 0, row + shift < major)

    def line_go(step):
        copies = []
        for way in (1, -1):
            copy = line_copy(step, way)
            leaves = jnp.logical_and(has(-way * (step - 1)), has(way))
            pl.when(leaves)(copy.start)
            sends.append((leaves, copy))
            copies.append((has(-way * step), copy))
        return copies

    def ring_go(block, own, present, step):
        pieces = (0, 1) if step == minor // 2 else (None, None)
        first = own and step == 1
        pair = (
            copy_of(on_ring(block, 1 - step), first, pieces[0], on_ring(row, 1)),
            copy_of(on_ring(block, step - 1), first, pieces[1], on_ring(row, -1)),
        )
        for copy in pair:
            when(present)(copy.start)
            sends.append((present, copy))
        return pair

    blocks = [(row, True, None)]
    flight = line_go(1)
    rings = [ring_go(row, True, None, 1)]
    between(0)
    for step in range(1, major):
        for present, copy in flight:
            pl.when(present)(copy.wait_recv)
        if step + 1 < major:
            flight = line_go(step + 1)
        for way in (1, -1):
            block = lax.rem(row - way * step + major, major)
            blocks.append((block, False, has(-way * step)))
            rings.append(ring_go(*blocks[-1], 1))
        between(step)
    for step in range(1, minor // 2 + 1):
        for i, (block, own, present) in enumerate(blocks):
            for copy in rings[i]:
                when(present)(copy.wait_recv)
            if step < minor // 2:
                rings[i] = ring_go(block, own, present, step + 1)
    return [(when(present), copy) for present, copy in sends]


def gather_kernel(n, w_ref, x_ref, w_out, y_ref, hold_w, hold_x, ws, wr, xs, xr, local):
    greet_table(n)
    me = lax.axis_index("table")
    depth = w_ref.shape[0]
    load = pltpu.make_async_copy(w_ref, hold_w, local.at[2])
    load.start()
    copies = exchange_copies(n, x_ref, y_ref, xs, xr, second_window)
    share = -(-(n - 1) // factors(n)[0])

    def between(i):
        for copy in copies[i * share : (i + 1) * share]:
            copy.start()

    started = start_gather(n, w_ref, w_out, ws, wr, between)
    load.wait()
    put = pltpu.make_async_copy(
        hold_w, w_out.at[pl.ds(pl.multiple_of(me * depth, depth), depth)], local.at[3]
    )
    put.start()
    store = own_block(x_ref, y_ref, hold_x, local, second_window)
    store.wait()
    put.wait()
    for copy in copies:
        copy.wait()
    for when, copy in started:
        when(copy.wait_send)


def gather_and_exchange(w, x, n, collective_id):
    steps = gather_steps(n)
    return pl.pallas_call(
        functools.partial(gather_kernel, n),
        out_shape=(
            jax.ShapeDtypeStruct((n * w.shape[0], w.shape[1]), w.dtype),
            jax.ShapeDtypeStruct(x.shape, x.dtype),
        ),
        in_specs=[ANY, ANY],
        out_specs=(ANY, ANY),
        scratch_shapes=[
            pltpu.VMEM(w.shape, w.dtype),
            pltpu.VMEM(x.shape[:1] + x.shape[2:], x.dtype),
            pltpu.SemaphoreType.DMA((steps,)),
            pltpu.SemaphoreType.DMA((steps,)),
            pltpu.SemaphoreType.DMA((n,)),
            pltpu.SemaphoreType.DMA((n,)),
            pltpu.SemaphoreType.DMA((4,)),
        ],
        compiler_params=pltpu.CompilerParams(
            collective_id=collective_id, has_side_effects=True
        ),
    )(w, x)


def greet_pair():
    other = 1 - lax.axis_index("mp")
    barrier = pltpu.get_barrier_semaphore()
    pl.semaphore_signal(barrier, inc=1, device_id={"mp": other}, device_id_type=MESH)
    pl.semaphore_wait(barrier, 1)
    return other


def join_kernel(x_ref, full_ref, send, recv, local):
    other = greet_pair()
    width = x_ref.shape[1]
    window = full_ref.at[:, pl.ds(pl.multiple_of((1 - other) * width, width), width)]
    copy = pltpu.make_async_remote_copy(
        src_ref=x_ref,
        dst_ref=window,
        send_sem=send,
        recv_sem=recv,
        device_id={"mp": other},
        device_id_type=MESH,
    )
    copy.start()
    keep = pltpu.make_async_copy(x_ref, window, local)
    keep.start()
    keep.wait()
    copy.wait()


def join_halves(x, collective_id):
    return pl.pallas_call(
        join_kernel,
        out_shape=jax.ShapeDtypeStruct((x.shape[0], 2 * x.shape[1]), x.dtype),
        in_specs=[pl.BlockSpec(memory_space=pltpu.VMEM)],
        out_specs=ANY,
        scratch_shapes=[pltpu.SemaphoreType.DMA] * 3,
        compiler_params=pltpu.CompilerParams(
            collective_id=collective_id, has_side_effects=True
        ),
    )(x)


def swap_kernel(part_ref, side_ref, part_out, side_out, send, recv):
    other = greet_pair()
    width = part_out.shape[1]
    copies = []
    pairs = (
        (part_ref.at[:, pl.ds(pl.multiple_of(other * width, width), width)], part_out),
        (side_ref, side_out),
    )
    for i, (src, dst) in enumerate(pairs):
        copy = pltpu.make_async_remote_copy(
            src_ref=src,
            dst_ref=dst,
            send_sem=send.at[i],
            recv_sem=recv.at[i],
            device_id={"mp": other},
            device_id_type=MESH,
        )
        copy.start()
        copies.append(copy)
    for copy in copies:
        copy.wait()


def swap_halves(part, side, collective_id):
    return pl.pallas_call(
        swap_kernel,
        out_shape=(
            jax.ShapeDtypeStruct((part.shape[0], part.shape[1] // 2), part.dtype),
            jax.ShapeDtypeStruct(side.shape, side.dtype),
        ),
        in_specs=[ANY, ANY],
        out_specs=(ANY, ANY),
        scratch_shapes=[pltpu.SemaphoreType.DMA((2,)), pltpu.SemaphoreType.DMA((2,))],
        compiler_params=pltpu.CompilerParams(
            collective_id=collective_id, has_side_effects=True
        ),
    )(part, side)


def on_device(
    hash_tables, byte_table, byte_ids, hash_owner, hash_offset, gain, proj_weight, cotangent
):
    groups = lax.axis_size("table")
    half = lax.axis_index("mp")
    ngram, rows_dev, width = hash_tables.shape
    tokens = byte_ids.shape[0]
    full_width = gain.shape[0]
    capacity = 2 * tokens // groups
    span = groups * capacity
    places = jnp.arange(span, dtype=jnp.int32)
    marks = []
    requests = []
    for k in range(ngram):
        owner = hash_owner[k, :, 0]
        slot = owner * capacity + slot_rank(owner, groups)
        mark = slot[:, None] == places[None, :]
        marks.append(mark)
        wanted = jnp.sum(jnp.where(mark, hash_offset[k][:, None] + 1, 0), axis=0) - 1
        requests.append(wanted.reshape(groups, capacity))
    stacked = jnp.stack(requests, axis=1)
    lanes = -(-capacity // 128) * 128
    levels = -(-ngram // 8) * 8
    stacked = jnp.pad(stacked, ((0, 0), (0, levels - ngram), (0, lanes - capacity)))
    asked = exchange(stacked, groups, first_window, 0)[:, :ngram, :capacity]
    asked = jnp.transpose(asked, (1, 0, 2)).reshape(ngram, span)
    rows = jnp.arange(rows_dev, dtype=jnp.int32)
    hits = (asked[:, :, None] == rows[None, None, :]).astype(jnp.bfloat16)
    looked = lax.dot_general(
        hits, hash_tables, (((2,), (1,)), ((0,), (0,))), preferred_element_type=jnp.float32
    ).astype(jnp.bfloat16)
    weight, fetched = gather_and_exchange(
        proj_weight, looked.reshape(ngram, groups, capacity, width), groups, 1
    )

    mark = jnp.concatenate(marks, axis=1).astype(jnp.bfloat16)
    codes = jnp.arange(byte_table.shape[0], dtype=jnp.int32)
    picks = (byte_ids[:, None] == codes[None, :]).astype(jnp.bfloat16)
    summed = jnp.dot(picks, byte_table, preferred_element_type=jnp.float32)
    summed = summed + jnp.dot(
        mark, fetched.reshape(ngram * span, width), preferred_element_type=jnp.float32
    )
    embedded_half = summed.astype(jnp.bfloat16)
    embedded = join_halves(embedded_half, 2)
    full = embedded.astype(jnp.float32)
    total = jnp.sum(full * full, axis=1)
    scale = lax.rsqrt(total / full_width + eps)[:, None]
    normed = (full * scale * gain[None, :]).astype(jnp.bfloat16)
    partial_grad = lax.dot_general(
        cotangent, weight, (((1,), (1,)), ((), ())), preferred_element_type=jnp.float32
    )
    inner_part = jnp.sum(full * (partial_grad * gain[None, :]), axis=1, keepdims=True)
    other_grad, other_inner = swap_halves(
        partial_grad, jnp.broadcast_to(inner_part, (tokens, 128)), 3
    )
    values = embedded_half.astype(jnp.float32)
    gain_half = lax.dynamic_slice_in_dim(gain, half * width, width)
    own_grad = lax.dynamic_slice_in_dim(partial_grad, half * width, width, axis=1)
    scaled = (own_grad + other_grad) * gain_half[None, :]
    inner = (inner_part + other_inner[:, :1]) / full_width
    dembed = (scale * scaled - values * scale * scale * scale * inner).astype(jnp.bfloat16)
    outgoing = lax.dot_general(
        mark, dembed, (((0,), (0,)), ((), ())), preferred_element_type=jnp.float32
    ).astype(jnp.bfloat16)
    arrived = lax.all_to_all(
        outgoing.reshape(ngram, groups, capacity, width),
        "table",
        split_axis=1,
        concat_axis=1,
        tiled=True,
    )
    grads = lax.dot_general(
        hits,
        arrived.reshape(ngram, span, width),
        (((1,), (1,)), ((0,), (0,))),
        preferred_element_type=jnp.float32,
    ).astype(jnp.bfloat16)
    projected = jnp.dot(normed, weight, preferred_element_type=jnp.float32).astype(jnp.bfloat16)
    return (projected, grads)


def solution(mesh):
    return jax.shard_map(
        on_device,
        mesh=mesh,
        in_specs=(
            P(None, "table", "mp"),
            P(None, "mp"),
            P("table"),
            P(None, "table", None),
            P(None, "table"),
            P(),
            P("table", "mp"),
            P("table", "mp"),
        ),
        out_specs=(P("table", "mp"), P(None, "table", "mp")),
        check_vma=False,
    )
```

```python
import functools

import jax
import jax.numpy as jnp
from jax import lax
from jax.experimental import pallas as pl
from jax.experimental.pallas import tpu as pltpu
from jax.sharding import PartitionSpec as P

eps = 1e-05
MESH = pl.DeviceIdType.MESH
ANY = pl.BlockSpec(memory_space=pl.ANY)


def slot_rank(owner, groups):
    marks = (owner[:, None] == jnp.arange(groups, dtype=jnp.int32)[None, :]).astype(jnp.int32)
    before = jnp.cumsum(marks, axis=0) - marks
    return jnp.sum(before * marks, axis=1)


def greet_table(n):
    me = lax.axis_index("table")
    barrier = pltpu.get_barrier_semaphore()
    for j in range(1, n):
        pl.semaphore_signal(
            barrier, inc=1, device_id={"table": lax.rem(me + j, n)}, device_id_type=MESH
        )
    pl.semaphore_wait(barrier, n - 1)


def exchange_copies(n, src, dst, send, recv, window):
    me = lax.axis_index("table")
    copies = []
    for j in range(1, n):
        to = lax.rem(me + j, n)
        copy = pltpu.make_async_remote_copy(
            src_ref=window(src, to),
            dst_ref=window(dst, me),
            send_sem=send.at[j],
            recv_sem=recv.at[j],
            device_id={"table": to},
            device_id_type=MESH,
        )
        copies.append(copy)
    return copies


def first_window(ref, d):
    return ref.at[d]


def factors(n):
    major = 1
    while major * major < n:
        major *= 2
    return major, n // major


def snake(i):
    return (i // 2) * 2 + (i % 2 + i // 2) % 2


def gather_steps(n):
    major, minor = factors(n)
    return 2 * (major - 1) + (2 * major - 1) * 2 * (minor // 2)


def start_gather(n, w_ref, out_ref, send, recv, between, done):
    major, minor = factors(n)
    me = lax.axis_index("table")
    row, place = me // minor, snake(me % minor)
    depth = w_ref.shape[0]
    spot = [0]
    sends = []

    def always(body):
        body()

    def when(condition):
        return always if condition is None else pl.when(condition)

    def on_ring(r, shift):
        return r * minor + snake(lax.rem(place + shift + minor, minor))

    def copy_of(origin, own, piece, to):
        size = depth if piece is None else depth // 2
        offset = 0 if piece is None else piece * size
        at = pl.ds(pl.multiple_of(origin * depth + offset, size), size)
        copy = pltpu.make_async_remote_copy(
            src_ref=w_ref.at[pl.ds(offset, size)] if own else out_ref.at[at],
            dst_ref=out_ref.at[at],
            send_sem=send.at[spot[0]],
            recv_sem=recv.at[spot[0]],
            device_id={"table": to},
            device_id_type=MESH,
        )
        spot[0] += 1
        return copy

    def line_copy(step, way):
        origin = lax.rem(row - way * (step - 1) + major, major)
        to = lax.rem(row + way + major, major)
        return copy_of(
            origin * minor + me % minor, step == 1, None, to * minor + me % minor
        )

    def has(shift):
        return jnp.logical_and(row + shift >= 0, row + shift < major)

    def line_go(step):
        copies = []
        for way in (1, -1):
            copy = line_copy(step, way)
            leaves = jnp.logical_and(has(-way * (step - 1)), has(way))
            pl.when(leaves)(copy.start)
            sends.append((leaves, copy))
            copies.append((has(-way * step), copy))
        return copies

    def ring_go(block, own, present, step):
        pieces = (0, 1) if step == minor // 2 else (None, None)
        first = own and step == 1
        pair = (
            copy_of(on_ring(block, 1 - step), first, pieces[0], on_ring(row, 1)),
            copy_of(on_ring(block, step - 1), first, pieces[1], on_ring(row, -1)),
        )
        for copy in pair:
            when(present)(copy.start)
            sends.append((present, copy))
        return pair

    blocks = [(row, True, None)]
    flight = line_go(1)
    rings = [ring_go(row, True, None, 1)]
    between(0)

    def forward(i, step):
        block, own, present = blocks[i]
        for copy in rings[i]:
            when(present)(copy.wait_recv)
        if step < minor // 2:
            rings[i] = ring_go(block, own, present, step + 1)
        else:
            when(present)(functools.partial(done, block))

    ready = 0
    for step in range(1, major):
        for present, copy in flight:
            pl.when(present)(copy.wait_recv)
        if step + 1 < major:
            flight = line_go(step + 1)
        known = len(blocks)
        for way in (1, -1):
            block = lax.rem(row - way * step + major, major)
            blocks.append((block, False, has(-way * step)))
            rings.append(ring_go(*blocks[-1], 1))
        between(step)
        if minor // 2 > 1:
            for i in range(ready, known):
                forward(i, 1)
            ready = known
    for step in range(1, minor // 2 + 1):
        for i in range(len(blocks)):
            if step > 1 or minor // 2 == 1 or i >= ready:
                forward(i, step)
    return [(when(present), copy) for present, copy in sends]


def rows_of(ref, d, capacity):
    return ref.at[:, pl.ds(pl.multiple_of(d * capacity, capacity), capacity)]


def gather_kernel(
    n, w_ref, asks_ref, table_ref, cot_ref,
    w_out, asked_out, y_ref, grad_ref,
    w_all, asked, table, looked, ws, wr, qs, qr, xs, xr, ts, local,
):
    greet_table(n)
    major, minor = factors(n)
    me = lax.axis_index("table")
    depth = w_ref.shape[0]
    ngram, rows, width = table_ref.shape
    capacity = looked.shape[1] // n
    own_rows = pl.ds(pl.multiple_of(me * depth, depth), depth)
    loads = [
        pltpu.make_async_copy(table_ref.at[k], table.at[k], ts.at[k]) for k in range(ngram)
    ]
    keep = pltpu.make_async_copy(w_ref, w_all.at[own_rows], local.at[0])
    questions = exchange_copies(n, asks_ref, asked, qs, qr, first_window)
    for copy in questions:
        copy.start()
    for load in loads:
        load.start()
    keep.start()
    asked[me] = asks_ref[me]

    near, far = [], []
    for along in range(major):
        for across in range(minor):
            if along == 0 and across == 0:
                continue
            to = lax.rem(me // minor + along, major) * minor + lax.rem(me + across, minor)
            spot = along * minor + across
            (far if along else near).append(
                pltpu.make_async_remote_copy(
                    src_ref=rows_of(looked, to, capacity),
                    dst_ref=rows_of(y_ref, me, capacity),
                    send_sem=xs.at[spot],
                    recv_sem=xr.at[spot],
                    device_id={"table": to},
                    device_id_type=MESH,
                )
            )
    mine = pltpu.make_async_copy(
        rows_of(looked, me, capacity), rows_of(y_ref, me, capacity), local.at[1]
    )
    group = 128 // capacity
    tile = width // 4

    def look_up():
        for copy in questions:
            copy.wait_recv()
        for load in loads:
            load.wait()
        for q in range(n // group):
            for k in range(ngram):
                wanted = asked[q * group, k : k + 1, :]
                for i in range(1, group):
                    wanted = wanted + asked[q * group + i, k : k + 1, :]
                place = lax.broadcasted_iota(jnp.int32, (rows, 128), 0) + 1
                hit = (place == wanted).astype(jnp.float32).astype(jnp.bfloat16)

                @pl.loop(0, 4)
                def _(c):
                    columns = pl.ds(pl.multiple_of(c * tile, tile), tile)
                    found = lax.dot_general(
                        hit,
                        table[k, :, columns],
                        (((0,), (0,)), ((), ())),
                        preferred_element_type=jnp.float32,
                    )
                    looked[k, q * 128 : (q + 1) * 128, columns] = found.astype(looked.dtype)

    def between(i):
        if i == 0:
            look_up()
            mine.start()
            for copy in near:
                copy.start()
        if i == major - 2:
            for copy in far:
                copy.start()

    span = minor * depth
    chunk = min(512, span)
    puts = []

    def done(block):
        at = pl.ds(pl.multiple_of(block * span, span), span)
        put = pltpu.make_async_copy(w_all.at[at], w_out.at[at], local.at[2 + block])
        put.start()

        @pl.loop(0, span // chunk)
        def _(c):
            some = pl.ds(pl.multiple_of(block * span + c * chunk, chunk), chunk)
            grad_ref[:, some] = lax.dot_general(
                cot_ref[...],
                w_all[some, :],
                (((1,), (1,)), ((), ())),
                preferred_element_type=jnp.float32,
            )

    keep.wait()
    started = start_gather(n, w_ref, w_all, ws, wr, between, done)
    for copy in questions:
        copy.wait_send()
    asked_out[...] = asked[...]
    mine.wait()
    for copy in near + far:
        copy.wait()
    for when, copy in started:
        when(copy.wait_send)
    for block in range(major):
        at = pl.ds(block * span, span)
        pltpu.make_async_copy(w_all.at[at], w_out.at[at], local.at[2 + block]).wait()


def gather_and_exchange(w, asks, table, cot, capacity, n, collective_id):
    steps = gather_steps(n)
    ngram, _, width = table.shape
    whole = pl.BlockSpec(memory_space=pltpu.VMEM)
    return pl.pallas_call(
        functools.partial(gather_kernel, n),
        out_shape=(
            jax.ShapeDtypeStruct((n * w.shape[0], w.shape[1]), w.dtype),
            jax.ShapeDtypeStruct(asks.shape, asks.dtype),
            jax.ShapeDtypeStruct((ngram, n * capacity, width), table.dtype),
            jax.ShapeDtypeStruct((cot.shape[0], n * w.shape[0]), jnp.float32),
        ),
        in_specs=[ANY, whole, ANY, whole],
        out_specs=(ANY, whole, ANY, whole),
        scratch_shapes=[
            pltpu.VMEM((n * w.shape[0], w.shape[1]), w.dtype),
            pltpu.VMEM(asks.shape, asks.dtype),
            pltpu.VMEM(table.shape, table.dtype),
            pltpu.VMEM((ngram, n * capacity, width), table.dtype),
            pltpu.SemaphoreType.DMA((steps,)),
            pltpu.SemaphoreType.DMA((steps,)),
            pltpu.SemaphoreType.DMA((n,)),
            pltpu.SemaphoreType.DMA((n,)),
            pltpu.SemaphoreType.DMA((n,)),
            pltpu.SemaphoreType.DMA((n,)),
            pltpu.SemaphoreType.DMA((ngram,)),
            pltpu.SemaphoreType.DMA((2 + factors(n)[0],)),
        ],
        compiler_params=pltpu.CompilerParams(
            collective_id=collective_id, has_side_effects=True
        ),
    )(w, asks, table, cot)


def greet_pair():
    other = 1 - lax.axis_index("mp")
    barrier = pltpu.get_barrier_semaphore()
    pl.semaphore_signal(barrier, inc=1, device_id={"mp": other}, device_id_type=MESH)
    pl.semaphore_wait(barrier, 1)
    return other


def join_kernel(x_ref, full_ref, send, recv, local):
    other = greet_pair()
    width = x_ref.shape[1]
    window = full_ref.at[:, pl.ds(pl.multiple_of((1 - other) * width, width), width)]
    copy = pltpu.make_async_remote_copy(
        src_ref=x_ref,
        dst_ref=window,
        send_sem=send,
        recv_sem=recv,
        device_id={"mp": other},
        device_id_type=MESH,
    )
    copy.start()
    keep = pltpu.make_async_copy(x_ref, window, local)
    keep.start()
    keep.wait()
    copy.wait()


def join_halves(x, collective_id):
    return pl.pallas_call(
        join_kernel,
        out_shape=jax.ShapeDtypeStruct((x.shape[0], 2 * x.shape[1]), x.dtype),
        in_specs=[pl.BlockSpec(memory_space=pltpu.VMEM)],
        out_specs=ANY,
        scratch_shapes=[pltpu.SemaphoreType.DMA] * 3,
        compiler_params=pltpu.CompilerParams(
            collective_id=collective_id, has_side_effects=True
        ),
    )(x)


def swap_kernel(part_ref, side_ref, part_out, side_out, send, recv):
    other = greet_pair()
    width = part_out.shape[1]
    copies = []
    pairs = (
        (part_ref.at[:, pl.ds(pl.multiple_of(other * width, width), width)], part_out),
        (side_ref, side_out),
    )
    for i, (src, dst) in enumerate(pairs):
        copy = pltpu.make_async_remote_copy(
            src_ref=src,
            dst_ref=dst,
            send_sem=send.at[i],
            recv_sem=recv.at[i],
            device_id={"mp": other},
            device_id_type=MESH,
        )
        copy.start()
        copies.append(copy)
    for copy in copies:
        copy.wait()


def swap_halves(part, side, collective_id):
    return pl.pallas_call(
        swap_kernel,
        out_shape=(
            jax.ShapeDtypeStruct((part.shape[0], part.shape[1] // 2), part.dtype),
            jax.ShapeDtypeStruct(side.shape, side.dtype),
        ),
        in_specs=[ANY, ANY],
        out_specs=(ANY, ANY),
        scratch_shapes=[pltpu.SemaphoreType.DMA((2,)), pltpu.SemaphoreType.DMA((2,))],
        compiler_params=pltpu.CompilerParams(
            collective_id=collective_id, has_side_effects=True
        ),
    )(part, side)


def on_device(
    hash_tables, byte_table, byte_ids, hash_owner, hash_offset, gain, proj_weight, cotangent
):
    groups = lax.axis_size("table")
    half = lax.axis_index("mp")
    ngram, rows_dev, width = hash_tables.shape
    tokens = byte_ids.shape[0]
    full_width = gain.shape[0]
    capacity = 2 * tokens // groups
    span = groups * capacity
    places = jnp.arange(span, dtype=jnp.int32)
    marks = []
    requests = []
    for k in range(ngram):
        owner = hash_owner[k, :, 0]
        slot = owner * capacity + slot_rank(owner, groups)
        mark = slot[:, None] == places[None, :]
        marks.append(mark)
        wanted = jnp.sum(jnp.where(mark, hash_offset[k][:, None] + 1, 0), axis=0)
        requests.append(wanted.reshape(groups, capacity))
    shared = 128 // capacity
    lane = jnp.arange(128, dtype=jnp.int32)
    stacked = jnp.tile(jnp.stack(requests, axis=1), (1, 1, shared))
    stacked = jnp.where(lane // capacity == lax.axis_index("table") % shared, stacked, 0)
    levels = -(-ngram // 8) * 8
    stacked = jnp.pad(stacked, ((0, 0), (0, levels - ngram), (0, 0)))
    weight, asked, fetched, partial_grad = gather_and_exchange(
        proj_weight, stacked, hash_tables, cotangent, capacity, groups, 1
    )
    asked = jnp.sum(asked.reshape(groups // shared, shared, levels, 128)[:, :, :ngram], axis=1) - 1
    asked = jnp.transpose(asked, (1, 0, 2)).reshape(ngram, span)
    rows = jnp.arange(rows_dev, dtype=jnp.int32)
    hits = (asked[:, :, None] == rows[None, None, :]).astype(jnp.bfloat16)

    mark = jnp.concatenate(marks, axis=1).astype(jnp.bfloat16)
    codes = jnp.arange(byte_table.shape[0], dtype=jnp.int32)
    picks = (byte_ids[:, None] == codes[None, :]).astype(jnp.bfloat16)
    summed = jnp.dot(picks, byte_table, preferred_element_type=jnp.float32)
    summed = summed + jnp.dot(
        mark, fetched.reshape(ngram * span, width), preferred_element_type=jnp.float32
    )
    embedded_half = summed.astype(jnp.bfloat16)
    embedded = join_halves(embedded_half, 2)
    full = embedded.astype(jnp.float32)
    total = jnp.sum(full * full, axis=1)
    scale = lax.rsqrt(total / full_width + eps)[:, None]
    normed = (full * scale * gain[None, :]).astype(jnp.bfloat16)
    inner_part = jnp.sum(full * (partial_grad * gain[None, :]), axis=1, keepdims=True)
    other_grad, other_inner = swap_halves(
        partial_grad, jnp.broadcast_to(inner_part, (tokens, 128)), 3
    )
    values = embedded_half.astype(jnp.float32)
    gain_half = lax.dynamic_slice_in_dim(gain, half * width, width)
    own_grad = lax.dynamic_slice_in_dim(partial_grad, half * width, width, axis=1)
    scaled = (own_grad + other_grad) * gain_half[None, :]
    inner = (inner_part + other_inner[:, :1]) / full_width
    dembed = (scale * scaled - values * scale * scale * scale * inner).astype(jnp.bfloat16)
    outgoing = lax.dot_general(
        mark, dembed, (((0,), (0,)), ((), ())), preferred_element_type=jnp.float32
    ).astype(jnp.bfloat16)
    arrived = lax.all_to_all(
        outgoing.reshape(ngram, groups, capacity, width),
        "table",
        split_axis=1,
        concat_axis=1,
        tiled=True,
    )
    grads = lax.dot_general(
        hits,
        arrived.reshape(ngram, span, width),
        (((1,), (1,)), ((0,), (0,))),
        preferred_element_type=jnp.float32,
    ).astype(jnp.bfloat16)
    projected = jnp.dot(normed, weight, preferred_element_type=jnp.float32).astype(jnp.bfloat16)
    return (projected, grads)


def solution(mesh):
    return jax.shard_map(
        on_device,
        mesh=mesh,
        in_specs=(
            P(None, "table", "mp"),
            P(None, "mp"),
            P("table"),
            P(None, "table", None),
            P(None, "table"),
            P(),
            P("table", "mp"),
            P("table", "mp"),
        ),
        out_specs=(P("table", "mp"), P(None, "table", "mp")),
        check_vma=False,
    )
```
